1024 devices in a mesh: slab: 64 (over y_lo, z, core), energy: 16 (over x, y_hi).
Axes of the slice: x: 4, y: 8 (y_hi: 4, y_lo: 2; y = y_hi * 2 + y_lo), z: 16, core: 2. Of those that a mesh axis runs over, the one named last changes fastest.
Arguments:
- energy: float32 [64], P('energy'), may hold values from -0.1 to 0.1
- onsite: float32 [8192, 128], P('slab'), may hold values from -1.2 to 0.08, as said below
- coupling: bfloat16 [8192, 128], P('slab'), may hold values from -0.140625 to 0.140625
- atom_of: int32 [8192], P('slab'), may hold values from 0 to 31
- strength: float32 [2048], P('slab'), may hold values from 0.5 to 1.5
- previous: bfloat16 [64, 2, 8192, 128], P('energy', None, 'slab'), may hold values from -0.29882812 to 0.29882812
- phonon_weight: float32 [4], replicated, may hold values from 0.01 to 0.05
- offsets: int32 [4], replicated, may hold values from 1 to 4, as said below
- in_flight: bfloat16 [32, 2, 8192, 128], P('energy', None, 'slab'), may hold values from -0.3 to 1.4, as said below
Outputs:
- green_last: bfloat16 [32, 2, 8192, 128], P('energy', None, 'slab')
- diagonal: float32 [64, 2, 8192], P('energy', None, 'slab')
The draws below stay inside these ranges and needn't reach their ends.
Inputs may be any that keep to these rules, and one draw needn't show every extreme that they name: The largest of the 4 offsets equals 4 in every draw. `onsite`: each 128 x 128 block is symmetric and its diagonal lies in -1.2 to -0.8. `in_flight`: in each 128 x 128 block the diagonal's real part lies in 0.7 to 1.4 and its imaginary part in -0.3 to -0.05.
All inputs are finite; a program needn't handle non-finite values.
Results may differ from the reference program's by a relative error of at most 0.0028.
The reference program's roundings to bfloat16 on the way count: a program that leaves them out, or rounds other values in their place, can miss the bound.
Values may be sent and summed in bfloat16 or wider, within the bound.
No kernel may reach another device: no remote copies, remote signals or barrier semaphores. Data moves between devices by JAX's collectives and lax.ppermute only.
A program may use at most 32 MiB of HBM per device.

```python
import math
import jax
import jax.numpy as jnp
from jax import lax

B = 128
ATOMS = 32
EB = 2
TICKS = 2
MODES = 4
OMAX = 4
E_DEV = 4
NE = 64
EB_ALL = 32
ROWS = 8192
SLAB_ATOMS = 2048
N_SLAB = 64
N_ENERGY = 16


def draw_onsite(key, part):
    blocks = ROWS // B
    noise_key = jax.random.fold_in(key, 11)
    level_key = jax.random.fold_in(key, 12)
    noise = jnp.clip(jax.random.normal(noise_key, (blocks, B, B), jnp.float32), -4.0, 4.0) * 0.013
    identity = jnp.eye(B, dtype=jnp.float32)
    symmetric = (noise + jnp.swapaxes(noise, 1, 2)) * 0.70710678 * (1.0 - identity)
    levels = jax.random.uniform(level_key, (blocks, B), jnp.float32, -1.2, -0.8)
    return (symmetric + levels[:, :, None] * identity).reshape(ROWS, B)


def draw_offsets(key, part):
    value_key = jax.random.fold_in(key, 21)
    order_key = jax.random.fold_in(key, 22)
    values = jax.random.randint(value_key, (MODES - 1,), 1, OMAX + 1, dtype=jnp.int32)
    values = jnp.concatenate([values, jnp.full((1,), OMAX, jnp.int32)])
    order = jax.random.permutation(order_key, MODES)
    return values[order].astype(jnp.int32)


def draw_in_flight(key, part):
    blocks = ROWS // B
    noise_key = jax.random.fold_in(key, 31)
    real_key = jax.random.fold_in(key, 32)
    imag_key = jax.random.fold_in(key, 33)
    noise = jnp.clip(jax.random.normal(noise_key, (EB_ALL, 2, blocks, B, B), jnp.float32), -5.0, 5.0) * 0.02
    identity = jnp.eye(B, dtype=jnp.float32)
    real_diag = jax.random.uniform(real_key, (EB_ALL, blocks, B), jnp.float32, 0.7, 1.395)
    imag_diag = jax.random.uniform(imag_key, (EB_ALL, blocks, B), jnp.float32, -0.295, -0.05)
    diag_parts = jnp.stack([real_diag, imag_diag], axis=1)
    whole = noise * (1.0 - identity) + diag_parts[..., None] * identity
    return whole.reshape(EB_ALL, 2, ROWS, B).astype(jnp.bfloat16)


def plant(result, stream_key, least, top_value):
    index_at = [jax.random.randint(jax.random.fold_in(stream_key, axis), (), 0, length) for axis, length in enumerate(result.shape)]
    widest = result.shape.index(max(result.shape))
    next_to = index_at[:widest] + [(index_at[widest] + 1) % result.shape[widest]] + index_at[widest + 1:]
    return result.at[tuple(index_at)].set(least).at[tuple(next_to)].set(top_value)


def shard_levels(key, shape, shards, low, largest):
    def one(axis_at, parts):
        heights = jax.random.uniform(jax.random.fold_in(jax.random.fold_in(key, 6), axis_at), (parts,), jnp.float32, low / len(shards), largest / len(shards))
        return jnp.repeat(jnp.exp(heights), shape[axis_at] // parts).reshape((-1,) + (1,) * (len(shape) - axis_at - 1))

    level = one(*shards[0])
    for cut in shards[1:]:
        level = level * one(*cut)
    return level


def normal_values(rng, shape, spread, limit, split=(), kind=jnp.bfloat16):
    gain = shard_levels(rng, shape, split, -0.22, 0.18) if split else 1.0
    drawn = jax.random.normal(rng, shape, jnp.float32) * spread * gain
    return jnp.minimum(jnp.maximum(drawn, -limit), limit).astype(kind)


def setup_inputs(seed: int = 0) -> dict:
    seeds = jax.random.split(jax.random.key(seed), 10)
    energy = jnp.clip(jax.random.uniform(seeds[0], (NE,), jnp.float32, -0.1, 0.1) * shard_levels(seeds[0], (NE,), ((0, 16),), -0.4, 0.0), -0.1, 0.1)
    onsite = draw_onsite(jax.random.fold_in(seeds[9], 71), 0)
    coupling = normal_values(seeds[2], (ROWS, B), (0.256 / B ** 0.5), 0.140625, ((0, 64),))
    atom_of = plant(jax.random.randint(seeds[3], (ROWS,), 0, ATOMS), jax.random.fold_in(seeds[3], 1), 0, ATOMS - 1).astype(jnp.int32)
    strength = jnp.clip(jnp.exp(math.log(1.5) - 1.0986123 * jax.random.uniform(seeds[4], (SLAB_ATOMS,), jnp.float32) ** shard_levels(seeds[4], (SLAB_ATOMS,), ((0, 64),), -0.2, 0.2)), 0.5, 1.5)
    previous = normal_values(seeds[5], (NE, 2, ROWS, B), 0.05, 0.29882812, ((0, 16), (2, 64)))
    phonon_weight = jnp.clip(jnp.exp(jax.random.uniform(seeds[6], (MODES,), jnp.float32, math.log(0.01), math.log(0.05))), 0.01, 0.05)
    offsets = draw_offsets(jax.random.fold_in(seeds[9], 71), 0)
    in_flight = draw_in_flight(jax.random.fold_in(seeds[9], 71), 0)
    return {"energy": energy, "onsite": onsite, "coupling": coupling, "atom_of": atom_of, "strength": strength, "previous": previous, "phonon_weight": phonon_weight, "offsets": offsets, "in_flight": in_flight}


broadening = 0.05


def full_product(left_side, right_side):
    return jnp.matmul(left_side.astype(jnp.float32), right_side.astype(jnp.float32), precision=lax.Precision.HIGHEST)


def complex_product(left_side, right_side):
    left_real = left_side[..., 0, :, :]
    left_imag = left_side[..., 1, :, :]
    right_real = right_side[..., 0, :, :]
    right_imag = right_side[..., 1, :, :]
    real_part = full_product(left_real, right_real) - full_product(left_imag, right_imag)
    imag_part = full_product(left_real, right_imag) + full_product(left_imag, right_real)
    return jnp.stack([real_part, imag_part], axis=-3)


def advance(incoming, coupling, onsite, self_energy, energies):
    identity = jnp.eye(B, dtype=jnp.float32)
    mixed_block = full_product(coupling, incoming).astype(jnp.bfloat16)
    coupled = full_product(mixed_block, jnp.swapaxes(coupling, -1, -2))
    shifted = energies[..., None, None] * identity - onsite
    real_part = shifted - self_energy[..., 0, :, :] - coupled[..., 0, :, :]
    imag_part = broadening * identity - self_energy[..., 1, :, :] - coupled[..., 1, :, :]
    level_gap = energies[..., None] - jnp.diagonal(onsite, axis1=-2, axis2=-1)
    denominator = level_gap * level_gap + broadening * broadening
    start_real = level_gap / denominator
    start_imag = -broadening / denominator
    scaled_real = real_part * start_real[..., None, :] - imag_part * start_imag[..., None, :]
    scaled_imag = real_part * start_imag[..., None, :] + imag_part * start_real[..., None, :]
    rest_real = 2.0 * identity - scaled_real
    rest_imag = -scaled_imag
    first_real = start_real[..., :, None] * rest_real - start_imag[..., :, None] * rest_imag
    first_imag = start_real[..., :, None] * rest_imag + start_imag[..., :, None] * rest_real
    system = jnp.stack([real_part, imag_part], axis=-3).astype(jnp.bfloat16)
    first_guess = jnp.stack([first_real, first_imag], axis=-3).astype(jnp.bfloat16)
    product = complex_product(system, first_guess)
    residue = jnp.stack([2.0 * identity - product[..., 0, :, :], -product[..., 1, :, :]], axis=-3).astype(jnp.bfloat16)
    return complex_product(first_guess, residue).astype(jnp.bfloat16)


def reference(energy, onsite, coupling, atom_of, strength, previous, phonon_weight, offsets, in_flight):
    onsite_blocks = onsite.reshape(N_SLAB, B, B)[:, None]
    coupling_blocks = coupling.reshape(N_SLAB, B, B)[:, None, None]
    matches = (atom_of.reshape(N_SLAB, B)[:, :, None] == jnp.arange(ATOMS, dtype=jnp.int32)[None, None, :]).astype(jnp.float32)
    orbital_scale = jnp.einsum("sba,sa->sb", matches, strength.reshape(N_SLAB, ATOMS), precision=lax.Precision.HIGHEST)
    pair_scale = orbital_scale[:, :, None] * orbital_scale[:, None, :]
    energy_groups = energy.reshape(N_ENERGY, E_DEV)
    flight_groups = in_flight.reshape(N_ENERGY, EB, 2, ROWS, B)
    slab_ids = jnp.arange(N_SLAB, dtype=jnp.int32)

    def energy_group(inputs):
        group_index, energies_dev, flight_blocks = inputs
        local_energy = group_index * E_DEV + jnp.arange(E_DEV, dtype=jnp.int32)
        phonon = jnp.zeros((E_DEV, 2, ROWS, B), jnp.float32)
        for member in range(MODES):
            below = local_energy - offsets[member]
            above = local_energy + offsets[member]
            inside_below = ((below >= 0) & (below < NE)).astype(jnp.float32)
            inside_above = ((above >= 0) & (above < NE)).astype(jnp.float32)
            lower_part = jnp.take(previous, jnp.clip(below, 0, NE - 1).astype(jnp.int32), axis=0).astype(jnp.float32) * inside_below[:, None, None, None]
            upper_part = jnp.take(previous, jnp.clip(above, 0, NE - 1).astype(jnp.int32), axis=0).astype(jnp.float32) * inside_above[:, None, None, None]
            phonon = phonon + phonon_weight[member] * (lower_part + upper_part)
        self_energy = phonon.reshape(E_DEV, 2, N_SLAB, B, B).transpose(2, 0, 1, 3, 4) * pair_scale[:, None, None]
        diagonals = jnp.zeros((N_SLAB, E_DEV, 2, B), jnp.float32)
        green_block = None
        for tick_index in range(TICKS):
            batch_order = jnp.mod(tick_index - slab_ids, TICKS)
            batch_rows = (batch_order[:, None] * EB + jnp.arange(EB, dtype=jnp.int32)[None, :]).astype(jnp.int32)
            self_batch = jnp.take_along_axis(self_energy, batch_rows[:, :, None, None, None], axis=1)
            energy_batch = energies_dev[batch_rows]
            if tick_index == 0:
                arriving = flight_blocks.reshape(EB, 2, N_SLAB, B, B).transpose(2, 0, 1, 3, 4)
            else:
                arriving = jnp.concatenate([jnp.zeros_like(green_block[:1]), green_block[:-1]], axis=0)
            green_block = advance(arriving, coupling_blocks, onsite_blocks, self_batch, energy_batch)
            green_diagonal = jnp.diagonal(green_block, axis1=-2, axis2=-1).astype(jnp.float32)
            diagonals = diagonals.at[slab_ids[:, None], batch_rows].set(green_diagonal)
        last_blocks = green_block.transpose(1, 2, 0, 3, 4).reshape(EB, 2, ROWS, B)
        diagonal_out = diagonals.transpose(1, 2, 0, 3).reshape(E_DEV, 2, ROWS)
        return last_blocks, diagonal_out

    last_blocks, diagonal_out = lax.map(energy_group, (jnp.arange(N_ENERGY, dtype=jnp.int32), energy_groups, flight_groups))
    return last_blocks.reshape(EB_ALL, 2, ROWS, B), diagonal_out.reshape(NE, 2, ROWS)
```

```python
import jax
import jax.numpy as jnp
from jax import lax
from jax.experimental import pallas as pl
from jax.experimental.pallas import tpu as pltpu
from jax.sharding import PartitionSpec as P

B = 128
ATOMS = 32
EB = 2
MODES = 4
OMAX = 4
E_DEV = 4
CHUNK = 32

broadening = 0.05
f32 = jnp.float32
bf16 = jnp.bfloat16

VMEM = pltpu.MemorySpace.VMEM
SMEM = pltpu.MemorySpace.SMEM


def offset_weights(weight_ref, offset_ref):
    sums = {}
    for distance in range(1, OMAX + 1):
        total = jnp.float32(0.0)
        for mode in range(MODES):
            total = total + jnp.where(offset_ref[mode] == distance, weight_ref[mode], 0.0)
        sums[distance] = total
    return sums


def weighted(terms):
    total = None
    for factor, value in terms:
        part = factor * value
        total = part if total is None else total + part
    return total


def partial_kernel(slab_ref, weight_ref, offset_ref, previous_ref, up0_ref, down0_ref, up1_ref, down1_ref):
    sums = offset_weights(weight_ref, offset_ref)

    def fill(ups, downs):
        for part in range(2):
            for row in range(0, B, CHUNK):
                rows = pl.ds(row, CHUNK)
                values = [previous_ref[e, part, rows, :].astype(f32) for e in range(E_DEV)]
                for target in range(E_DEV):
                    up = weighted([(sums[OMAX + target - e], values[e]) for e in range(target, E_DEV)])
                    down = weighted([(sums[e + OMAX - target], values[e]) for e in range(0, target + 1)])
                    ups[target // EB][target % EB, part, rows, :] = up.astype(bf16)
                    downs[target // EB][target % EB, part, rows, :] = down.astype(bf16)

    parity = slab_ref[0]

    @pl.when(parity == 0)
    def _():
        fill((up0_ref, up1_ref), (down0_ref, down1_ref))

    @pl.when(parity != 0)
    def _():
        fill((up1_ref, up0_ref), (down1_ref, down0_ref))


def mixed_coupling(coupling, blocks):
    wide = jnp.concatenate(blocks, axis=1)
    mixed = jnp.dot(coupling, wide, preferred_element_type=f32).astype(bf16)
    tall = jnp.concatenate([mixed[:, i * B : (i + 1) * B] for i in range(len(blocks))], axis=0)
    both = lax.dot_general(tall, coupling, (((1,), (1,)), ((), ())), preferred_element_type=f32)
    return [both[i * B : (i + 1) * B, :] for i in range(len(blocks))]


def diagonal_mask():
    return lax.broadcasted_iota(jnp.int32, (B, B), 0) == lax.broadcasted_iota(jnp.int32, (B, B), 1)


def local_kernel(
    slab_ref, weight_ref, offset_ref, energy_ref, onsite_ref, coupling_ref, atom_ref, strength_ref,
    previous_ref, flight_ref, base_ref, product_ref, twice_ref, pair_ref,
):
    sums = offset_weights(weight_ref, offset_ref)
    on_diagonal = diagonal_mask()
    atoms = lax.broadcasted_iota(jnp.int32, (ATOMS, ATOMS), 0) == lax.broadcasted_iota(jnp.int32, (ATOMS, ATOMS), 1)
    strength_column = jnp.sum(jnp.where(atoms, strength_ref[...], 0.0), axis=1, keepdims=True)
    matches = lax.broadcasted_iota(jnp.int32, (ATOMS, B), 0) == atom_ref[...]
    scale_row = jnp.sum(jnp.where(matches, strength_column, 0.0), axis=0, keepdims=True)
    scale_column = jnp.sum(jnp.where(on_diagonal, scale_row, 0.0), axis=1, keepdims=True)
    pair_ref[...] = scale_column * scale_row

    level_row = jnp.sum(jnp.where(on_diagonal, onsite_ref[...], 0.0), axis=0, keepdims=True)
    level_column = jnp.sum(jnp.where(on_diagonal, onsite_ref[...], 0.0), axis=1, keepdims=True)

    def start(gap):
        denominator = gap * gap + broadening * broadening
        return gap / denominator, -broadening / denominator

    for e in range(E_DEV):
        row_real, row_imag = start(energy_ref[e] - level_row)
        column_real, column_imag = start(energy_ref[e] - level_column)
        product_ref[e, 0] = column_real * row_real - column_imag * row_imag
        product_ref[e, 1] = column_real * row_imag + column_imag * row_real
        twice_ref[e, 0:1, :] = 2.0 * row_real
        twice_ref[e, 1:2, :] = 2.0 * row_imag

    for row in range(0, B, CHUNK):
        rows = pl.ds(row, CHUNK)
        pair = pair_ref[rows, :]
        mask = (lax.broadcasted_iota(jnp.int32, (CHUNK, B), 0) + row) == lax.broadcasted_iota(jnp.int32, (CHUNK, B), 1)
        onsite = onsite_ref[rows, :]
        for part in range(2):
            values = [previous_ref[e, part, rows, :].astype(f32) for e in range(E_DEV)]
            for target in range(E_DEV):
                phonon = weighted([(sums[abs(target - e)], values[e]) for e in range(E_DEV) if e != target])
                if part == 0:
                    head = jnp.where(mask, energy_ref[target], 0.0) - onsite
                else:
                    head = jnp.where(mask, jnp.float32(broadening), 0.0)
                base_ref[target, part, rows, :] = head - phonon * pair

    first = slab_ref[0] * EB
    coupled = mixed_coupling(coupling_ref[...], [flight_ref[m, c] for m in range(EB) for c in range(2)])
    for m in range(EB):
        for c in range(2):
            base_ref[first + m, c] = base_ref[first + m, c] - coupled[m * 2 + c]


def complex_rows(real, imag):
    return jnp.concatenate([real, imag], axis=1)


def complex_square(real, imag):
    top = jnp.concatenate([real, imag], axis=1)
    bottom = jnp.concatenate([-imag, real], axis=1)
    return jnp.concatenate([top, bottom], axis=0)


def green_of(real, imag, product_real, product_imag, twice_real, twice_imag, on_diagonal):
    first_real = jnp.where(on_diagonal, twice_real, 0.0) - (real * product_real - imag * product_imag)
    first_imag = jnp.where(on_diagonal, twice_imag, 0.0) - (real * product_imag + imag * product_real)
    first_real = first_real.astype(bf16)
    first_imag = first_imag.astype(bf16)
    product = jnp.dot(
        complex_rows(real.astype(bf16), imag.astype(bf16)), complex_square(first_real, first_imag),
        preferred_element_type=f32,
    )
    residue_real = (jnp.where(on_diagonal, 2.0, 0.0) - product[:, :B]).astype(bf16)
    residue_imag = (-product[:, B:]).astype(bf16)
    green = jnp.dot(
        complex_rows(first_real, first_imag), complex_square(residue_real, residue_imag),
        preferred_element_type=f32,
    ).astype(bf16)
    return green[:, :B], green[:, B:]


def green_diagonal(green, on_diagonal):
    return jnp.sum(jnp.where(on_diagonal, green.astype(f32), 0.0), axis=0, keepdims=True)


def first_tick_kernel(slab_ref, base_ref, product_ref, twice_ref, pair_ref, low_ref, high_ref, green_ref, diagonal_ref):
    first = slab_ref[0] * EB
    on_diagonal = diagonal_mask()
    pair = pair_ref[...]
    for m in range(EB):
        e = first + m
        system = [
            base_ref[e, c] - (low_ref[m, c].astype(f32) + high_ref[m, c].astype(f32)) * pair for c in range(2)
        ]
        greens = green_of(
            system[0], system[1], product_ref[e, 0], product_ref[e, 1],
            twice_ref[e, 0:1, :], twice_ref[e, 1:2, :], on_diagonal,
        )
        for c in range(2):
            green_ref[m, c] = greens[c]
            diagonal_ref[m, c : c + 1, :] = green_diagonal(greens[c], on_diagonal)


def last_tick_kernel(
    slab_ref, base_ref, product_ref, twice_ref, pair_ref, low_ref, high_ref, arriving_ref, coupling_ref,
    earlier_ref, green_ref, diagonal_ref,
):
    earlier = slab_ref[0] * EB
    first = (1 - slab_ref[0]) * EB
    on_diagonal = diagonal_mask()
    pair = pair_ref[...]
    coupled = mixed_coupling(coupling_ref[...], [arriving_ref[m, c] for m in range(EB) for c in range(2)])
    for m in range(EB):
        e = first + m
        system = [
            base_ref[e, c]
            - (low_ref[m, c].astype(f32) + high_ref[m, c].astype(f32)) * pair
            - coupled[m * 2 + c]
            for c in range(2)
        ]
        greens = green_of(
            system[0], system[1], product_ref[e, 0], product_ref[e, 1],
            twice_ref[e, 0:1, :], twice_ref[e, 1:2, :], on_diagonal,
        )
        diagonal_ref[earlier + m] = earlier_ref[m]
        for c in range(2):
            green_ref[m, c] = greens[c]
            diagonal_ref[e, c : c + 1, :] = green_diagonal(greens[c], on_diagonal)


def spec(space):
    return pl.BlockSpec(memory_space=space)


def call(kernel, scalars, arrays, outs, name):
    return pl.pallas_call(
        kernel,
        in_specs=[spec(SMEM)] * len(scalars) + [spec(VMEM)] * len(arrays),
        out_specs=[spec(VMEM)] * len(outs),
        out_shape=[jax.ShapeDtypeStruct(shape, dtype) for shape, dtype in outs],
        name=name,
    )(*scalars, *arrays)


def body(energy, onsite, coupling, atom_of, strength, previous, phonon_weight, offsets, in_flight):
    parity = (lax.axis_index("slab") & 1).astype(jnp.int32).reshape(1)
    devices = lax.axis_size("energy")
    up = [(i, i + 1) for i in range(devices - 1)]
    down = [(i + 1, i) for i in range(devices - 1)]
    slabs = lax.axis_size("slab")
    onward = [(i, i + 1) for i in range(slabs - 1)]
    half = (EB, 2, B, B)

    up0, down0, up1, down1 = call(
        partial_kernel, (parity, phonon_weight, offsets), (previous,), [(half, bf16)] * 4, "partials"
    )
    low0 = lax.ppermute(up0, "energy", up)
    high0 = lax.ppermute(down0, "energy", down)
    low1 = lax.ppermute(up1, "energy", up)
    high1 = lax.ppermute(down1, "energy", down)
    base, product, twice, pair = call(
        local_kernel,
        (parity, phonon_weight, offsets, energy),
        (onsite, coupling, atom_of.reshape(1, B), strength.reshape(1, ATOMS), previous, in_flight),
        [((E_DEV, 2, B, B), f32), ((E_DEV, 2, B, B), f32), ((E_DEV, 2, B), f32), ((B, B), f32)],
        "local",
    )
    green0, diagonal0 = call(
        first_tick_kernel, (parity,), (base, product, twice, pair, low0, high0),
        [(half, bf16), ((EB, 2, B), f32)], "first_tick",
    )
    arriving = lax.ppermute(green0, "slab", onward)
    green1, diagonals = call(
        last_tick_kernel, (parity,),
        (base, product, twice, pair, low1, high1, arriving, coupling, diagonal0),
        [(half, bf16), ((E_DEV, 2, B), f32)], "last_tick",
    )
    return green1, diagonals


def solution(mesh):
    placed = (
        P("energy"),
        P("slab", None),
        P("slab", None),
        P("slab"),
        P("slab"),
        P("energy", None, "slab", None),
        P(),
        P(),
        P("energy", None, "slab", None),
    )
    return jax.shard_map(
        body,
        mesh=mesh,
        in_specs=placed,
        out_specs=(P("energy", None, "slab", None), P("energy", None, "slab")),
        check_vma=False,
    )
```

```python
import jax
import jax.numpy as jnp
from jax import lax
from jax.experimental import pallas as pl
from jax.experimental.pallas import tpu as pltpu
from jax.sharding import PartitionSpec as P

B = 128
ATOMS = 32
EB = 2
MODES = 4
OMAX = 4
E_DEV = 4
CHUNK = 32

broadening = 0.05
f32 = jnp.float32
bf16 = jnp.bfloat16

VMEM = pltpu.MemorySpace.VMEM


def slab_parity():
    return lax.axis_index("slab") & 1


def offset_weights(weight_ref, offset_ref):
    sums = {}
    for distance in range(1, OMAX + 1):
        hits = jnp.where(offset_ref[...] == distance, weight_ref[...], 0.0)
        sums[distance] = jnp.sum(hits, axis=1, keepdims=True)
    return sums


def weighted(terms):
    total = None
    for factor, value in terms:
        part = factor * value
        total = part if total is None else total + part
    return total


def fill_partials(batch, sums, previous_ref, up_ref, down_ref):
    for part in range(2):
        for row in range(0, B, CHUNK):
            rows = pl.ds(row, CHUNK)
            values = [previous_ref[e, part, rows, :].astype(f32) for e in range(E_DEV)]
            for m in range(EB):
                target = batch * EB + m
                up = weighted([(sums[OMAX + target - e], values[e]) for e in range(target, E_DEV)])
                down = weighted([(sums[e + OMAX - target], values[e]) for e in range(0, target + 1)])
                up_ref[m, part, rows, :] = up.astype(bf16)
                down_ref[m, part, rows, :] = down.astype(bf16)


def tick_partials(tick, sums, previous_ref, up_ref, down_ref):
    parity = slab_parity()
    for batch in range(2):

        @pl.when(parity == (batch ^ tick))
        def _():
            fill_partials(batch, sums, previous_ref, up_ref, down_ref)


def opening_kernel(*refs):
    count = (len(refs) - 3) // 2
    inputs, (up_ref, down_ref), kept, semaphores = refs[:count], refs[count : count + 2], refs[count + 2 : -1], refs[-1]
    copies = [pltpu.make_async_copy(inputs[i], kept[i], semaphores.at[i]) for i in range(count)]
    for copy in copies:
        copy.start()
    for copy in copies[:3]:
        copy.wait()
    previous_ref, weight_ref, offset_ref = kept[:3]
    tick_partials(0, offset_weights(weight_ref, offset_ref), previous_ref, up_ref, down_ref)
    for copy in copies[3:]:
        copy.wait()


def mixed_coupling(coupling, blocks):
    wide = jnp.concatenate(blocks, axis=1)
    mixed = jnp.dot(coupling, wide, preferred_element_type=f32).astype(bf16)
    tall = jnp.concatenate([mixed[:, i * B : (i + 1) * B] for i in range(len(blocks))], axis=0)
    both = lax.dot_general(tall, coupling, (((1,), (1,)), ((), ())), preferred_element_type=f32)
    return [both[i * B : (i + 1) * B, :] for i in range(len(blocks))]


def diagonal_mask():
    return lax.broadcasted_iota(jnp.int32, (B, B), 0) == lax.broadcasted_iota(jnp.int32, (B, B), 1)


def local_kernel(
    previous_ref, weight_ref, offset_ref, flight_ref, onsite_ref, coupling_ref, energy_ref, atom_ref, strength_ref,
    up_ref, down_ref, base_ref, product_ref, twice_ref, pair_ref,
):
    sums = offset_weights(weight_ref, offset_ref)
    tick_partials(1, sums, previous_ref, up_ref, down_ref)
    on_diagonal = diagonal_mask()
    atoms = lax.broadcasted_iota(jnp.int32, (ATOMS, ATOMS), 0) == lax.broadcasted_iota(jnp.int32, (ATOMS, ATOMS), 1)
    strength_column = jnp.sum(jnp.where(atoms, strength_ref[...], 0.0), axis=1, keepdims=True)
    matches = lax.broadcasted_iota(jnp.int32, (ATOMS, B), 0) == atom_ref[...]
    scale_row = jnp.sum(jnp.where(matches, strength_column, 0.0), axis=0, keepdims=True)
    scale_column = jnp.sum(jnp.where(on_diagonal, scale_row, 0.0), axis=1, keepdims=True)
    pair_ref[...] = scale_column * scale_row

    level_row = jnp.sum(jnp.where(on_diagonal, onsite_ref[...], 0.0), axis=0, keepdims=True)
    level_column = jnp.sum(jnp.where(on_diagonal, onsite_ref[...], 0.0), axis=1, keepdims=True)

    def start(gap):
        denominator = gap * gap + broadening * broadening
        return gap / denominator, -broadening / denominator

    for e in range(E_DEV):
        row_real, row_imag = start(energy_ref[:, e : e + 1] - level_row)
        column_real, column_imag = start(energy_ref[:, e : e + 1] - level_column)
        product_ref[e, 0] = column_real * row_real - column_imag * row_imag
        product_ref[e, 1] = column_real * row_imag + column_imag * row_real
        twice_ref[e, 0:1, :] = 2.0 * row_real
        twice_ref[e, 1:2, :] = 2.0 * row_imag

    for row in range(0, B, CHUNK):
        rows = pl.ds(row, CHUNK)
        pair = pair_ref[rows, :]
        mask = (lax.broadcasted_iota(jnp.int32, (CHUNK, B), 0) + row) == lax.broadcasted_iota(jnp.int32, (CHUNK, B), 1)
        onsite = onsite_ref[rows, :]
        for part in range(2):
            values = [previous_ref[e, part, rows, :].astype(f32) for e in range(E_DEV)]
            for target in range(E_DEV):
                phonon = weighted([(sums[abs(target - e)], values[e]) for e in range(E_DEV) if e != target])
                if part == 0:
                    head = jnp.where(mask, energy_ref[:, target : target + 1], 0.0) - onsite
                else:
                    head = jnp.where(mask, jnp.float32(broadening), 0.0)
                base_ref[target, part, rows, :] = head - phonon * pair

    first = slab_parity() * EB
    coupled = mixed_coupling(coupling_ref[...], [flight_ref[m, c] for m in range(EB) for c in range(2)])
    for m in range(EB):
        for c in range(2):
            base_ref[first + m, c] = base_ref[first + m, c] - coupled[m * 2 + c]


def complex_rows(real, imag):
    return jnp.concatenate([real, imag], axis=1)


def complex_square(real, imag):
    top = jnp.concatenate([real, imag], axis=1)
    bottom = jnp.concatenate([-imag, real], axis=1)
    return jnp.concatenate([top, bottom], axis=0)


def green_of(real, imag, product_real, product_imag, twice_real, twice_imag, on_diagonal):
    first_real = jnp.where(on_diagonal, twice_real, 0.0) - (real * product_real - imag * product_imag)
    first_imag = jnp.where(on_diagonal, twice_imag, 0.0) - (real * product_imag + imag * product_real)
    first_real = first_real.astype(bf16)
    first_imag = first_imag.astype(bf16)
    product = jnp.dot(
        complex_rows(real.astype(bf16), imag.astype(bf16)), complex_square(first_real, first_imag),
        preferred_element_type=f32,
    )
    residue_real = (jnp.where(on_diagonal, 2.0, 0.0) - product[:, :B]).astype(bf16)
    residue_imag = (-product[:, B:]).astype(bf16)
    green = jnp.dot(
        complex_rows(first_real, first_imag), complex_square(residue_real, residue_imag),
        preferred_element_type=f32,
    ).astype(bf16)
    return green[:, :B], green[:, B:]


def green_diagonal(green, on_diagonal):
    return jnp.sum(jnp.where(on_diagonal, green.astype(f32), 0.0), axis=0, keepdims=True)


def first_tick_kernel(base_ref, product_ref, twice_ref, pair_ref, low_ref, high_ref, green_ref, diagonal_ref):
    first = slab_parity() * EB
    on_diagonal = diagonal_mask()
    pair = pair_ref[...]
    for m in range(EB):
        e = first + m
        system = [
            base_ref[e, c] - (low_ref[m, c].astype(f32) + high_ref[m, c].astype(f32)) * pair for c in range(2)
        ]
        greens = green_of(
            system[0], system[1], product_ref[e, 0], product_ref[e, 1],
            twice_ref[e, 0:1, :], twice_ref[e, 1:2, :], on_diagonal,
        )
        for c in range(2):
            green_ref[m, c] = greens[c]
            diagonal_ref[m, c : c + 1, :] = green_diagonal(greens[c], on_diagonal)


def last_tick_kernel(
    base_ref, product_ref, twice_ref, pair_ref, low_ref, high_ref, arriving_ref, coupling_ref,
    earlier_ref, green_ref, diagonal_ref,
):
    earlier = slab_parity() * EB
    first = (1 - slab_parity()) * EB
    on_diagonal = diagonal_mask()
    pair = pair_ref[...]
    coupled = mixed_coupling(coupling_ref[...], [arriving_ref[m, c] for m in range(EB) for c in range(2)])
    for m in range(EB):
        e = first + m
        system = [
            base_ref[e, c]
            - (low_ref[m, c].astype(f32) + high_ref[m, c].astype(f32)) * pair
            - coupled[m * 2 + c]
            for c in range(2)
        ]
        greens = green_of(
            system[0], system[1], product_ref[e, 0], product_ref[e, 1],
            twice_ref[e, 0:1, :], twice_ref[e, 1:2, :], on_diagonal,
        )
        diagonal_ref[earlier + m] = earlier_ref[m]
        for c in range(2):
            green_ref[m, c] = greens[c]
            diagonal_ref[e, c : c + 1, :] = green_diagonal(greens[c], on_diagonal)


def call(kernel, arrays, outs, name, kept=True):
    arrays = [pltpu.with_memory_space_constraint(array, VMEM) for array in arrays]
    shapes = [VMEM(shape, dtype) if kept else jax.ShapeDtypeStruct(shape, dtype) for shape, dtype in outs]
    space = pl.BlockSpec(memory_space=VMEM)
    return pl.pallas_call(
        kernel,
        in_specs=[space] * len(arrays),
        out_specs=[space] * len(outs),
        out_shape=shapes,
        name=name,
    )(*arrays)


def body(energy, onsite, coupling, atom_of, strength, previous, phonon_weight, offsets, in_flight):
    devices = lax.axis_size("energy")
    up = [(i, i + 1) for i in range(devices - 1)]
    down = [(i + 1, i) for i in range(devices - 1)]
    slabs = lax.axis_size("slab")
    onward = [(i, i + 1) for i in range(slabs - 1)]
    half = (EB, 2, B, B)
    arrays = (
        previous, phonon_weight.reshape(1, MODES), offsets.reshape(1, MODES), in_flight, onsite, coupling,
        energy.reshape(1, E_DEV), atom_of.reshape(1, B), strength.reshape(1, ATOMS),
    )
    up0, down0, *kept = pl.pallas_call(
        opening_kernel,
        in_specs=[pl.BlockSpec(memory_space=pl.ANY)] * len(arrays),
        out_specs=[pl.BlockSpec(memory_space=VMEM)] * (len(arrays) + 2),
        out_shape=[VMEM(half, bf16)] * 2 + [VMEM(array.shape, array.dtype) for array in arrays],
        scratch_shapes=[pltpu.SemaphoreType.DMA((len(arrays),))],
        name="opening",
    )(*arrays)
    low0 = lax.ppermute(up0, "energy", up)
    high0 = lax.ppermute(down0, "energy", down)
    up1, down1, base, product, twice, pair = call(
        local_kernel,
        kept,
        [(half, bf16)] * 2
        + [((E_DEV, 2, B, B), f32), ((E_DEV, 2, B, B), f32), ((E_DEV, 2, B), f32), ((B, B), f32)],
        "local",
    )
    low1 = lax.ppermute(up1, "energy", up)
    high1 = lax.ppermute(down1, "energy", down)
    green0, diagonal0 = call(
        first_tick_kernel, (base, product, twice, pair, low0, high0), [(half, bf16), ((EB, 2, B), f32)], "first_tick"
    )
    arriving = lax.ppermute(green0, "slab", onward)
    green1, diagonals = call(
        last_tick_kernel,
        (base, product, twice, pair, low1, high1, arriving, kept[5], diagonal0),
        [(half, bf16), ((E_DEV, 2, B), f32)], "last_tick", kept=False,
    )
    return green1, diagonals


def solution(mesh):
    placed = (
        P("energy"),
        P("slab", None),
        P("slab", None),
        P("slab"),
        P("slab"),
        P("energy", None, "slab", None),
        P(),
        P(),
        P("energy", None, "slab", None),
    )
    return jax.shard_map(
        body,
        mesh=mesh,
        in_specs=placed,
        out_specs=(P("energy", None, "slab", None), P("energy", None, "slab")),
        check_vma=False,
    )
```

```python
import functools

import jax
import jax.numpy as jnp
from jax import lax
from jax.experimental import pallas as pl
from jax.experimental.pallas import tpu as pltpu
from jax.sharding import PartitionSpec as P

B = 128
ATOMS = 32
EB = 2
MODES = 4
OMAX = 4
E_DEV = 4
CHUNK = 32

broadening = 0.05
f32 = jnp.float32
bf16 = jnp.bfloat16

VMEM = pltpu.MemorySpace.VMEM


def slab_parity():
    return lax.axis_index("slab") & 1


def offset_weights(weight_ref, offset_ref):
    sums = {}
    for distance in range(1, OMAX + 1):
        hits = jnp.where(offset_ref[...] == distance, weight_ref[...], 0.0)
        sums[distance] = jnp.sum(hits, axis=1, keepdims=True)
    return sums


def weighted(terms):
    total = None
    for factor, value in terms:
        part = factor * value
        total = part if total is None else total + part
    return total


def fill_partials(batch, sums, previous_ref, up_ref, down_ref):
    for part in range(2):
        for row in range(0, B, CHUNK):
            rows = pl.ds(row, CHUNK)
            values = [previous_ref[e, part, rows, :].astype(f32) for e in range(E_DEV)]
            for m in range(EB):
                target = batch * EB + m
                up = weighted([(sums[OMAX + target - e], values[e]) for e in range(target, E_DEV)])
                down = weighted([(sums[e + OMAX - target], values[e]) for e in range(0, target + 1)])
                up_ref[m, part, rows, :] = up.astype(bf16)
                down_ref[m, part, rows, :] = down.astype(bf16)


def tick_partials(tick, sums, previous_ref, up_ref, down_ref):
    parity = slab_parity()
    for batch in range(2):

        @pl.when(parity == (batch ^ tick))
        def _():
            fill_partials(batch, sums, previous_ref, up_ref, down_ref)


def opening_kernel(*refs):
    count = (len(refs) - 5) // 2
    inputs, outs, kept, semaphores = refs[:count], refs[count : count + 4], refs[count + 4 : -1], refs[-1]
    copies = [pltpu.make_async_copy(inputs[i], kept[i], semaphores.at[i]) for i in range(count)]
    for copy in copies:
        copy.start()
    for copy in copies[:3]:
        copy.wait()
    previous_ref, weight_ref, offset_ref = kept[:3]
    sums = offset_weights(weight_ref, offset_ref)
    for tick in range(2):
        tick_partials(tick, sums, previous_ref, outs[2 * tick], outs[2 * tick + 1])
    for copy in copies[3:]:
        copy.wait()


def mixed_coupling(coupling, blocks):
    wide = jnp.concatenate(blocks, axis=1)
    mixed = jnp.dot(coupling, wide, preferred_element_type=f32).astype(bf16)
    tall = jnp.concatenate([mixed[:, i * B : (i + 1) * B] for i in range(len(blocks))], axis=0)
    both = lax.dot_general(tall, coupling, (((1,), (1,)), ((), ())), preferred_element_type=f32)
    return [both[i * B : (i + 1) * B, :] for i in range(len(blocks))]


def diagonal_mask():
    return lax.broadcasted_iota(jnp.int32, (B, B), 0) == lax.broadcasted_iota(jnp.int32, (B, B), 1)


def local_kernel(
    previous_ref, weight_ref, offset_ref, flight_ref, onsite_ref, coupling_ref, energy_ref, atom_ref, strength_ref,
    base_ref, product_ref, twice_ref, pair_ref,
):
    sums = offset_weights(weight_ref, offset_ref)
    on_diagonal = diagonal_mask()
    atoms = lax.broadcasted_iota(jnp.int32, (ATOMS, ATOMS), 0) == lax.broadcasted_iota(jnp.int32, (ATOMS, ATOMS), 1)
    strength_column = jnp.sum(jnp.where(atoms, strength_ref[...], 0.0), axis=1, keepdims=True)
    matches = lax.broadcasted_iota(jnp.int32, (ATOMS, B), 0) == atom_ref[...]
    scale_row = jnp.sum(jnp.where(matches, strength_column, 0.0), axis=0, keepdims=True)
    scale_column = jnp.sum(jnp.where(on_diagonal, scale_row, 0.0), axis=1, keepdims=True)
    pair_ref[...] = scale_column * scale_row

    level_row = jnp.sum(jnp.where(on_diagonal, onsite_ref[...], 0.0), axis=0, keepdims=True)
    level_column = jnp.sum(jnp.where(on_diagonal, onsite_ref[...], 0.0), axis=1, keepdims=True)

    def start(gap):
        denominator = gap * gap + broadening * broadening
        return gap / denominator, -broadening / denominator

    for e in range(E_DEV):
        row_real, row_imag = start(energy_ref[:, e : e + 1] - level_row)
        column_real, column_imag = start(energy_ref[:, e : e + 1] - level_column)
        product_ref[e, 0] = column_real * row_real - column_imag * row_imag
        product_ref[e, 1] = column_real * row_imag + column_imag * row_real
        twice_ref[e, 0:1, :] = 2.0 * row_real
        twice_ref[e, 1:2, :] = 2.0 * row_imag

    for row in range(0, B, CHUNK):
        rows = pl.ds(row, CHUNK)
        pair = pair_ref[rows, :]
        mask = (lax.broadcasted_iota(jnp.int32, (CHUNK, B), 0) + row) == lax.broadcasted_iota(jnp.int32, (CHUNK, B), 1)
        onsite = onsite_ref[rows, :]
        for part in range(2):
            values = [previous_ref[e, part, rows, :].astype(f32) for e in range(E_DEV)]
            for target in range(E_DEV):
                phonon = weighted([(sums[abs(target - e)], values[e]) for e in range(E_DEV) if e != target])
                if part == 0:
                    head = jnp.where(mask, energy_ref[:, target : target + 1], 0.0) - onsite
                else:
                    head = jnp.where(mask, jnp.float32(broadening), 0.0)
                base_ref[target, part, rows, :] = head - phonon * pair

    first = slab_parity() * EB
    coupled = mixed_coupling(coupling_ref[...], [flight_ref[m, c] for m in range(EB) for c in range(2)])
    for m in range(EB):
        for c in range(2):
            base_ref[first + m, c] = base_ref[first + m, c] - coupled[m * 2 + c]


def complex_rows(real, imag):
    return jnp.concatenate([real, imag], axis=1)


def complex_square(real, imag):
    top = jnp.concatenate([real, imag], axis=1)
    bottom = jnp.concatenate([-imag, real], axis=1)
    return jnp.concatenate([top, bottom], axis=0)


def green_of(real, imag, product_real, product_imag, twice_real, twice_imag, on_diagonal):
    first_real = jnp.where(on_diagonal, twice_real, 0.0) - (real * product_real - imag * product_imag)
    first_imag = jnp.where(on_diagonal, twice_imag, 0.0) - (real * product_imag + imag * product_real)
    first_real = first_real.astype(bf16)
    first_imag = first_imag.astype(bf16)
    product = jnp.dot(
        complex_rows(real.astype(bf16), imag.astype(bf16)), complex_square(first_real, first_imag),
        preferred_element_type=f32,
    )
    residue_real = (jnp.where(on_diagonal, 2.0, 0.0) - product[:, :B]).astype(bf16)
    residue_imag = (-product[:, B:]).astype(bf16)
    green = jnp.dot(
        complex_rows(first_real, first_imag), complex_square(residue_real, residue_imag),
        preferred_element_type=f32,
    ).astype(bf16)
    return green[:, :B], green[:, B:]


def green_diagonal(green, on_diagonal):
    return jnp.sum(jnp.where(on_diagonal, green.astype(f32), 0.0), axis=0, keepdims=True)


def halo_sum(refs, m, c):
    total = None
    for ref, index in refs:
        value = ref[index + (m, c)].astype(f32)
        total = value if total is None else total + value
    return total


def first_tick_kernel(indices, *refs):
    base_ref, product_ref, twice_ref, pair_ref = refs[:4]
    halos = list(zip(refs[4:-2], indices))
    green_ref, diagonal_ref = refs[-2:]

    first = slab_parity() * EB
    on_diagonal = diagonal_mask()
    pair = pair_ref[...]
    for m in range(EB):
        e = first + m
        system = [
            base_ref[e, c] - halo_sum(halos, m, c) * pair for c in range(2)
        ]
        greens = green_of(
            system[0], system[1], product_ref[e, 0], product_ref[e, 1],
            twice_ref[e, 0:1, :], twice_ref[e, 1:2, :], on_diagonal,
        )
        for c in range(2):
            green_ref[m, c] = greens[c]
            diagonal_ref[m, c : c + 1, :] = green_diagonal(greens[c], on_diagonal)


def last_tick_kernel(indices, *refs):
    base_ref, product_ref, twice_ref, pair_ref = refs[:4]
    halos = list(zip(refs[4:-5], indices))
    arriving_ref, coupling_ref, earlier_ref, green_ref, diagonal_ref = refs[-5:]
    earlier = slab_parity() * EB
    first = (1 - slab_parity()) * EB
    on_diagonal = diagonal_mask()
    pair = pair_ref[...]
    coupled = mixed_coupling(coupling_ref[...], [arriving_ref[m, c] for m in range(EB) for c in range(2)])
    for m in range(EB):
        e = first + m
        system = [
            base_ref[e, c]
            - halo_sum(halos, m, c) * pair
            - coupled[m * 2 + c]
            for c in range(2)
        ]
        greens = green_of(
            system[0], system[1], product_ref[e, 0], product_ref[e, 1],
            twice_ref[e, 0:1, :], twice_ref[e, 1:2, :], on_diagonal,
        )
        diagonal_ref[earlier + m] = earlier_ref[m]
        for c in range(2):
            green_ref[m, c] = greens[c]
            diagonal_ref[e, c : c + 1, :] = green_diagonal(greens[c], on_diagonal)


def call(kernel, arrays, outs, kept=True):
    arrays = [pltpu.with_memory_space_constraint(array, VMEM) for array in arrays]
    shapes = [VMEM(shape, dtype) if kept else jax.ShapeDtypeStruct(shape, dtype) for shape, dtype in outs]
    space = pl.BlockSpec(memory_space=VMEM)
    return pl.pallas_call(
        kernel, in_specs=[space] * len(arrays), out_specs=[space] * len(outs), out_shape=shapes
    )(*arrays)


def body(energy, onsite, coupling, atom_of, strength, previous, phonon_weight, offsets, in_flight):
    devices = lax.axis_size("energy")
    slabs = lax.axis_size("slab")
    onward = [(i, i + 1) for i in range(slabs - 1)]
    half = (EB, 2, B, B)
    arrays = (
        previous, phonon_weight.reshape(1, MODES), offsets.reshape(1, MODES), in_flight, onsite, coupling,
        energy.reshape(1, E_DEV), atom_of.reshape(1, B), strength.reshape(1, ATOMS),
    )
    up0, down0, up1, down1, *kept = pl.pallas_call(
        opening_kernel,
        in_specs=[pl.BlockSpec(memory_space=pl.ANY)] * len(arrays),
        out_specs=[pl.BlockSpec(memory_space=VMEM)] * (len(arrays) + 4),
        out_shape=[VMEM(half, bf16)] * 4 + [VMEM(array.shape, array.dtype) for array in arrays],
        scratch_shapes=[pltpu.SemaphoreType.DMA((len(arrays),))],
        name="opening",
    )(*arrays)
    energies = devices

    def halo_pairs(step, chosen):
        return [
            (s * energies + j, s * energies + j + step)
            for s in range(slabs)
            if chosen(s)
            for j in range(energies)
            if 0 <= j + step < energies
        ]

    last = slabs // 2 - 1

    def exchange(up_block, down_block, chosen):
        both = ("slab", "energy")
        low = lax.ppermute(up_block, both, halo_pairs(1, chosen))
        high = lax.ppermute(down_block, both, halo_pairs(-1, chosen))
        return low, high

    def send_onward(block):
        return lax.ppermute(block, "slab", onward)

    def is_last(s):
        return s == last

    def is_other(s):
        return s != last

    def local_work():
        return call(
            local_kernel, kept,
            [((E_DEV, 2, B, B), f32), ((E_DEV, 2, B, B), f32), ((E_DEV, 2, B), f32), ((B, B), f32)],
        )

    def first_tick(local, halos):
        arrays, indices = zip(*halos)
        return call(functools.partial(first_tick_kernel, indices), (*local, *arrays), [(half, bf16), ((EB, 2, B), f32)])

    def last_tick(local, halos, arriving):
        arrays, indices = zip(*halos)
        return call(
            functools.partial(last_tick_kernel, indices), (*local, *arrays, arriving, kept[5], diagonal0),
            [(half, bf16), ((E_DEV, 2, B), f32)], kept=False,
        )

    a = exchange(up0, down0, is_last)
    b = exchange(up0, down0, is_other)
    local = local_work()
    b1 = exchange(up1, down1, is_other)
    green0, diagonal0 = first_tick(local, [(x, ()) for x in a + b])
    arriving = send_onward(green0)
    c1 = exchange(up1, down1, is_last)
    late = [(x, ()) for x in b1 + c1]
    green1, diagonals = last_tick(local, late, arriving)
    return green1, diagonals


def solution(mesh):
    placed = (
        P("energy"),
        P("slab", None),
        P("slab", None),
        P("slab"),
        P("slab"),
        P("energy", None, "slab", None),
        P(),
        P(),
        P("energy", None, "slab", None),
    )

    return jax.shard_map(
        body,
        mesh=mesh,
        in_specs=placed,
        out_specs=(P("energy", None, "slab", None), P("energy", None, "slab")),
        check_vma=False,
    )
```
